32 devices in a mesh: dp: 16 (over z, x, core), tensor: 2 (over y).
Axes of the slice: x: 2, y: 2, z: 4, core: 2. Of those that a mesh axis runs over, the one named last changes fastest.
Arguments:
- tokens_in: bfloat16 [32768, 640], P(('dp', 'tensor')), may hold values from -6 to 6
- positions: int32 [32768], P('dp'), may hold values from 0 to 6142, as said below
- gain_attn_in: bfloat16 [640], P('dp'), may hold values from 0.25 to 1.75
- w_query: bfloat16 [640, 1024], P('dp', 'tensor'), may hold values from -0.25 to 0.25
- w_key: bfloat16 [640, 256], P('dp'), may hold values from -0.25 to 0.25
- w_value: bfloat16 [640, 256], P('dp'), may hold values from -0.25 to 0.25
- gain_query: bfloat16 [256], P('dp'), may hold values from 0.25 to 1.75
- gain_key: bfloat16 [256], P('dp'), may hold values from 0.25 to 1.75
- w_output: bfloat16 [1024, 640], P('tensor', 'dp'), may hold values from -0.1875 to 0.1875
- gain_attn_post: bfloat16 [640], P('dp'), may hold values from 0.25 to 1.75
- gain_ff_in: bfloat16 [640], P('dp'), may hold values from 0.25 to 1.75
- w_gate: bfloat16 [640, 2048], P('dp', 'tensor'), may hold values from -0.25 to 0.25
- w_up: bfloat16 [640, 2048], P('dp', 'tensor'), may hold values from -0.25 to 0.25
- w_down: bfloat16 [2048, 640], P('tensor', 'dp'), may hold values from -0.125 to 0.125
- gain_ff_post: bfloat16 [640], P('dp'), may hold values from 0.25 to 1.75
- cotangent: bfloat16 [32768, 640], P(('dp', 'tensor')), may hold values from -6 to 6
Outputs:
- out: bfloat16 [32768, 640], P(('dp', 'tensor'))
- grad_tokens: float32 [32768, 640], P(('dp', 'tensor'))
- grad_gain_attn_in: float32 [640], P('dp')
- grad_w_query: float32 [640, 1024], P('dp', 'tensor')
- grad_w_key: float32 [640, 256], P('dp')
- grad_w_value: float32 [640, 256], P('dp')
- grad_gain_query: float32 [256], P('dp')
- grad_gain_key: float32 [256], P('dp')
- grad_w_output: float32 [1024, 640], P('tensor', 'dp')
- grad_gain_attn_post: float32 [640], P('dp')
- grad_gain_ff_in: float32 [640], P('dp')
- grad_w_gate: float32 [640, 2048], P('dp', 'tensor')
- grad_w_up: float32 [640, 2048], P('dp', 'tensor')
- grad_w_down: float32 [2048, 640], P('tensor', 'dp')
- grad_gain_ff_post: float32 [640], P('dp')
The draws below stay inside these ranges and needn't reach their ends.
Inputs may be any that keep to these rules, and one draw needn't show every extreme that they name: `positions`: within each sequence of 2048 consecutive tokens a position is one more than the one before, except where a document begins, where it is 0; the first document of a sequence may begin at any position below 4096. In some sequence the first document begins at 4095 and fills the whole sequence.
All inputs are finite; a program needn't handle non-finite values.
Results may differ from the reference program's by a relative error of at most 0.017.
Values may be sent and summed in bfloat16 or wider, within the bound.
No kernel may reach another device: no remote copies, remote signals or barrier semaphores. Data moves between devices by JAX's collectives and lax.ppermute only.
A program may use at most 128 MiB of HBM per device.

```python
import math
import jax
import jax.numpy as jnp
from jax import lax

D = 640
HEADS = 4
HD = 256
FF = 2048
WINDOW = 512
HQ = 1024
SEQ = 2048
TOKENS = 32768


def draw_positions(key, part):
    seq_count = TOKENS // SEQ
    offset_key = jax.random.fold_in(key, 11)
    break_key = jax.random.fold_in(key, 23)
    chosen_key = jax.random.fold_in(key, 37)
    offsets = jax.random.randint(offset_key, (seq_count, 1), 0, 2 * SEQ)
    breaks = jax.random.randint(break_key, (seq_count, SEQ), 0, max(SEQ // 3, 2)) == 0
    chosen = jax.random.randint(chosen_key, (), 0, seq_count)
    is_chosen = jnp.arange(seq_count, dtype=jnp.int32)[:, None] == chosen
    offsets = jnp.where(is_chosen, 2 * SEQ - 1, offsets)
    breaks = breaks & jnp.logical_not(is_chosen)
    token_index = jnp.broadcast_to(jnp.arange(SEQ, dtype=jnp.int32)[None, :], (seq_count, SEQ))
    begins = lax.cummax(jnp.where(breaks, token_index, -1), axis=1)
    places = jnp.where(begins >= 0, token_index - begins, offsets + token_index)
    return places.reshape(TOKENS).astype(jnp.int32)


def strengthened(values, rng, source, target, parts, factor):
    def block_of(dim):
        return (jnp.arange(values.shape[dim]) // (values.shape[dim] // parts)).reshape((-1,) + (1,) * (values.ndim - 1 - dim))

    first = jax.random.permutation(rng, parts)[block_of(target)]
    far = (block_of(target) + parts // 2) % parts
    return jnp.where((block_of(source) == first) | (block_of(source) == far), factor * values, values)


def block_levels(own_key, shape, shards, least, largest):
    loudness = 1.0
    for dim, blocks in shards:
        steps = jax.random.uniform(jax.random.fold_in(jax.random.fold_in(own_key, 6), dim), (blocks,), jnp.float32, least / len(shards), largest / len(shards))
        loudness = loudness * jnp.repeat(jnp.exp(steps), shape[dim] // blocks).reshape((-1,) + (1,) * (len(shape) - 1 - dim))
    return loudness


def noise(stream_key, dims, deviation, most, shards=(), kind=jnp.bfloat16):
    level = block_levels(stream_key, dims, shards, -0.22, 0.18) if shards else 1.0
    values = jax.random.normal(stream_key, dims, jnp.float32) * deviation * level
    return jnp.minimum(jnp.maximum(values, -most), most).astype(kind)


def bell_draw_with(stream_key, extent, width, bound, cuts, heavy, kind=jnp.bfloat16):
    values = width * jax.random.normal(stream_key, extent, jnp.float32)
    if cuts:
        values = values * block_levels(stream_key, extent, cuts, -0.22, 0.18)
    return jnp.clip(strengthened(values, jax.random.fold_in(stream_key, 3), *heavy), -bound, bound).astype(kind)


def setup_inputs(seed: int = 0) -> dict:
    seeds = jax.random.split(jax.random.key(seed), 17)
    tokens_in = bell_draw_with(seeds[0], (TOKENS, D), 1.0, 6.0, ((0, 32),), (0, 1, 32, 2.75))
    positions = draw_positions(jax.random.fold_in(seeds[16], 71), 0)
    gain_attn_in = jnp.clip(1.0 + 0.15 * jax.random.normal(seeds[2], (D,), jnp.float32), 0.25, 1.75).astype(jnp.bfloat16)
    w_query = noise(seeds[3], (D, HQ), D ** -0.5, 0.25, ((0, 16), (1, 2)))
    w_key = noise(seeds[4], (D, HD), D ** -0.5, 0.25, ((0, 16),))
    w_value = noise(seeds[5], (D, HD), D ** -0.5, 0.25, ((0, 16),))
    gain_query = jnp.clip(1.0 + 0.15 * jax.random.normal(seeds[6], (HD,), jnp.float32), 0.25, 1.75).astype(jnp.bfloat16)
    gain_key = jnp.clip(1.0 + 0.15 * jax.random.normal(seeds[7], (HD,), jnp.float32), 0.25, 1.75).astype(jnp.bfloat16)
    w_output = noise(seeds[8], (HQ, D), HQ ** -0.5, 0.1875, ((0, 2), (1, 16)))
    gain_attn_post = jnp.clip(1.0 + 0.15 * jax.random.normal(seeds[9], (D,), jnp.float32), 0.25, 1.75).astype(jnp.bfloat16)
    gain_ff_in = jnp.clip(1.0 + 0.15 * jax.random.normal(seeds[10], (D,), jnp.float32), 0.25, 1.75).astype(jnp.bfloat16)
    w_gate = noise(seeds[11], (D, FF), D ** -0.5, 0.25, ((0, 16), (1, 2)))
    w_up = noise(seeds[12], (D, FF), D ** -0.5, 0.25, ((0, 16), (1, 2)))
    w_down = noise(seeds[13], (FF, D), FF ** -0.5, 0.125, ((0, 2), (1, 16)))
    gain_ff_post = jnp.clip(1.0 + 0.15 * jax.random.normal(seeds[14], (D,), jnp.float32), 0.25, 1.75).astype(jnp.bfloat16)
    cotangent = bell_draw_with(seeds[15], (TOKENS, D), 1.0, 6.0, ((0, 32),), (0, 1, 32, 2.75))
    return {"tokens_in": tokens_in, "positions": positions, "gain_attn_in": gain_attn_in, "w_query": w_query, "w_key": w_key, "w_value": w_value, "gain_query": gain_query, "gain_key": gain_key, "w_output": w_output, "gain_attn_post": gain_attn_post, "gain_ff_in": gain_ff_in, "w_gate": w_gate, "w_up": w_up, "w_down": w_down, "gain_ff_post": gain_ff_post, "cotangent": cotangent}


NORM_EPS = 1e-06
ROPE_BASE = 10000.0
MASK_FILL = -1e+30

@jax.custom_vjp
def low(v):
    return lax.optimization_barrier(v.astype(jnp.bfloat16)).astype(jnp.float32)

@jax.custom_vjp
def low_back(v):
    return v

def low_keep(v):
    return (low(v), None)

def low_pass(kept, grad):
    return (grad,)

def back_keep(v):
    return (v, None)

def back_low(kept, grad):
    return (low(grad),)
low.defvjp(low_keep, low_pass)
low_back.defvjp(back_keep, back_low)

def rms_norm(values, scale_gain):
    return values * lax.rsqrt(lax.optimization_barrier(jnp.mean(values * values, axis=-1, keepdims=True)) + NORM_EPS) * scale_gain

def rotate(values, cosine, sine_table):
    half_size = values.shape[-1] // 2
    first_half = values[..., :half_size]
    second = values[..., half_size:]
    return jnp.concatenate([first_half * cosine - second * sine_table, second * cosine + first_half * sine_table], axis=-1)

def rope_tables(places):
    freq_index = jnp.arange(HD // 2, dtype=jnp.float32)
    inverse = jnp.exp(freq_index * (-2.0 * math.log(ROPE_BASE) / HD))
    angles = places.astype(jnp.float32)[:, None] * inverse[None, :]
    return (jnp.cos(angles), jnp.sin(angles))

def window_mask(places, first_row, block_rows):
    flat_places = places.astype(jnp.int32)
    padded = jnp.concatenate([jnp.zeros((WINDOW,), jnp.int32), flat_places])
    query_place = lax.dynamic_slice_in_dim(flat_places, first_row, block_rows)
    key_place = lax.dynamic_slice_in_dim(padded, first_row, block_rows + WINDOW)
    query_index = first_row + jnp.arange(block_rows, dtype=jnp.int32)
    key_index = first_row - WINDOW + jnp.arange(block_rows + WINDOW, dtype=jnp.int32)
    distance = query_index[:, None] - key_index[None, :]
    return (key_index[None, :] >= 0) & (distance >= 0) & (distance < WINDOW) & (query_place[:, None] - key_place[None, :] == distance)

def attention(queries, keys_rot, values_low, places):
    seq_len = queries.shape[0]
    block_rows = min(512, seq_len)
    zero_rows = jnp.zeros((WINDOW, HD), queries.dtype)
    key_pad = jnp.concatenate([zero_rows, keys_rot], axis=0)
    value_pad = jnp.concatenate([zero_rows, values_low], axis=0)

    def one_block(block_index):
        first_row = block_index * block_rows
        query_block = lax.dynamic_slice_in_dim(queries, first_row, block_rows, 0)
        key_block = lax.dynamic_slice_in_dim(key_pad, first_row, block_rows + WINDOW, 0)
        value_block = lax.dynamic_slice_in_dim(value_pad, first_row, block_rows + WINDOW, 0)
        scores = low_back(jnp.einsum('qhd,kd->hqk', query_block, key_block, precision=lax.Precision.HIGHEST) * HD ** (-0.5))
        visible = window_mask(places, first_row, block_rows)
        scores = jnp.where(visible[None], scores, MASK_FILL)
        attn_probs = jnp.exp(scores - jax.nn.logsumexp(scores, axis=-1, keepdims=True))
        return jnp.einsum('hqk,kd->qhd', low(attn_probs), value_block, precision=lax.Precision.HIGHEST)
    blocks = lax.map(jax.checkpoint(one_block), jnp.arange(seq_len // block_rows, dtype=jnp.int32))
    return blocks.reshape(seq_len, HEADS * HD)

def layer_forward(rows_in, layer_weights, places):
    gain_in, w_query, w_key, w_value, query_gain, key_gain, w_output, post_gain, ff_gain, w_gate, w_up, w_down, ff_post_gain = layer_weights
    seq_len = rows_in.shape[0]
    cosine, sine_table = rope_tables(places)
    normed = low(rms_norm(rows_in, gain_in))
    query_raw = low_back(jnp.dot(normed, w_query, precision=lax.Precision.HIGHEST)).reshape(seq_len, HEADS, HD)
    key_raw = low_back(jnp.dot(normed, w_key, precision=lax.Precision.HIGHEST))
    values_low = low(low_back(jnp.dot(normed, w_value, precision=lax.Precision.HIGHEST)))
    queries = low(rotate(rms_norm(query_raw, query_gain), cosine[:, None, :], sine_table[:, None, :]))
    keys_rot = low(rotate(rms_norm(key_raw, key_gain), cosine, sine_table))
    mixed = low(low_back(attention(queries, keys_rot, values_low, places)))
    branch = low_back(jnp.dot(mixed, w_output, precision=lax.Precision.HIGHEST))
    middle = rows_in + rms_norm(branch, post_gain)
    normed_ff = low(rms_norm(middle, ff_gain))
    gate_vals = low_back(jnp.dot(normed_ff, w_gate, precision=lax.Precision.HIGHEST))
    up_vals = low_back(jnp.dot(normed_ff, w_up, precision=lax.Precision.HIGHEST))
    hidden = low(jax.nn.gelu(gate_vals, approximate=True) * up_vals)
    branch_ff = low_back(jnp.dot(hidden, w_down, precision=lax.Precision.HIGHEST))
    return middle + rms_norm(branch_ff, ff_post_gain)

def reference(tokens_in, positions, gain_attn_in, w_query, w_key, w_value, gain_query, gain_key, w_output, gain_attn_post, gain_ff_in, w_gate, w_up, w_down, gain_ff_post, cotangent):
    layer_weights = tuple((source.astype(jnp.float32) for source in (gain_attn_in, w_query, w_key, w_value, gain_query, gain_key, w_output, gain_attn_post, gain_ff_in, w_gate, w_up, w_down, gain_ff_post)))
    seq_count = tokens_in.shape[0] // SEQ
    inputs = tokens_in.astype(jnp.float32).reshape(seq_count, SEQ, D)
    cotangents = cotangent.astype(jnp.float32).reshape(seq_count, SEQ, D)
    all_places = positions.astype(jnp.int32).reshape(seq_count, SEQ)

    def one_sequence(carried, seq_item):
        seq_rows, seq_cot, seq_places = seq_item

        def forward(rows_in, *weight_list):
            return layer_forward(rows_in, weight_list, seq_places)
        result, pullback = jax.vjp(forward, seq_rows, *layer_weights)
        gradients = pullback(seq_cot)
        carried = tuple((running + fresh for running, fresh in zip(carried, gradients[1:])))
        return (carried, (result, gradients[0]))
    zero_init = tuple((jnp.zeros_like(source) for source in layer_weights))
    totals, (outputs, grad_rows) = lax.scan(one_sequence, zero_init, (inputs, cotangents, all_places))
    return (outputs.reshape(seq_count * SEQ, D).astype(jnp.bfloat16), grad_rows.reshape(seq_count * SEQ, D), totals[0], totals[1], totals[2], totals[3], totals[4], totals[5], totals[6], totals[7], totals[8], totals[9], totals[10], totals[11], totals[12])
```

```python
import functools
import math

import jax
import jax.numpy as jnp
from jax import lax
from jax.experimental import pallas as pl
from jax.experimental.pallas import tpu as pltpu
from jax.sharding import PartitionSpec as P

HD = 256
WINDOW = 512
NORM_EPS = 1e-06
ROPE_BASE = 10000.0
BF = jnp.bfloat16
F32 = jnp.float32


def rms_norm(values, scale_gain):
    return (
        values
        * lax.rsqrt(jnp.mean(values * values, axis=-1, keepdims=True) + NORM_EPS)
        * scale_gain
    )


def geglu(gate_vals, up_vals):
    return jax.nn.gelu(gate_vals, approximate=True) * up_vals


def rotate(values, cosine, sine_table):
    half_size = values.shape[-1] // 2
    first_half = values[..., :half_size]
    second = values[..., half_size:]
    return jnp.concatenate(
        [first_half * cosine - second * sine_table, second * cosine + first_half * sine_table],
        axis=-1,
    )


def rope_tables(places):
    freq_index = jnp.arange(HD // 2, dtype=F32)
    inverse = jnp.exp(freq_index * (-2.0 * math.log(ROPE_BASE) / HD))
    angles = places.astype(F32)[:, None] * inverse[None, :]
    return (jnp.cos(angles), jnp.sin(angles))


def dot(a, b):
    return jnp.dot(a, b, preferred_element_type=F32)


def dot_nt(a, b):
    return lax.dot_general(a, b, (((1,), (1,)), ((), ())), preferred_element_type=F32)


def dot_tn(a, b):
    return lax.dot_general(a, b, (((0,), (0,)), ((), ())), preferred_element_type=F32)


class Wires:
    def __init__(self, dp_size, tensor_size):
        self.dp_size = dp_size
        self.tensor_size = tensor_size
        self.dp_bits = dp_size.bit_length() - 1
        self.t_bits = tensor_size.bit_length() - 1
        self.count = dp_size * tensor_size

    def swap(self, values, bit):
        axis, size, mask = bit[0], self.dp_size, 1 << bit[1]
        if axis == "tensor":
            size = self.tensor_size
        return lax.ppermute(values, axis, [(i, i ^ mask) for i in range(size)])

    def orders(self):
        far = [("dp", b) for b in range(self.dp_bits - 1, 1, -1)]
        near = [("dp", 1)] if self.dp_bits > 1 else []
        core = [("dp", 0)] if self.dp_bits > 0 else []
        cross = [("tensor", b) for b in range(self.t_bits)]
        return far + near + cross + core, far + cross + near + core

    def places(self, order):
        slot = jnp.arange(self.count, dtype=jnp.int32)
        dp_rel = jnp.zeros_like(slot)
        t_rel = jnp.zeros_like(slot)
        for position, (axis, b) in enumerate(order):
            value = ((slot >> position) & 1) << b
            if axis == "dp":
                dp_rel = dp_rel | value
            else:
                t_rel = t_rel | value
        return (
            dp_rel ^ lax.axis_index("dp").astype(jnp.int32),
            t_rel ^ lax.axis_index("tensor").astype(jnp.int32),
        )


def gather_blocks(wires, block, order, parts):
    dp_of, t_of = wires.places(order)
    held = block[None]
    for bit in order[:-1]:
        held = jnp.concatenate([held, wires.swap(held, bit)], axis=0)
    other = wires.swap(held, order[-1])
    half = held.shape[0]
    rows, width = block.shape

    def body(dp_ref, t_ref, a_ref, b_ref, *outs):
        step = pl.program_id(0)

        def put(src):
            at = 0
            for (cols, _), out in zip(parts, outs):
                out[0] = src[0, :, at : at + cols]
                at += cols

        @pl.when(step < half)
        def _():
            put(a_ref)

        @pl.when(step >= half)
        def _():
            put(b_ref)

    out_specs, out_shape = [], []
    for cols, split in parts:
        if split:
            out_specs.append(pl.BlockSpec((1, rows, cols), lambda i, d, t: (d[i], 0, t[i])))
            shape = (wires.dp_size, rows, cols * wires.tensor_size)
        else:
            out_specs.append(pl.BlockSpec((1, rows, cols), lambda i, d, t: (d[i], 0, 0)))
            shape = (wires.dp_size, rows, cols)
        out_shape.append(jax.ShapeDtypeStruct(shape, block.dtype))
    outs = pl.pallas_call(
        body,
        grid_spec=pltpu.PrefetchScalarGridSpec(
            num_scalar_prefetch=2,
            grid=(2 * half,),
            in_specs=[
                pl.BlockSpec((1, rows, width), lambda i, d, t: (jnp.minimum(i, half - 1), 0, 0)),
                pl.BlockSpec((1, rows, width), lambda i, d, t: (jnp.maximum(i - half, 0), 0, 0)),
            ],
            out_specs=out_specs,
        ),
        out_shape=out_shape,
        cost_estimate=pl.CostEstimate(
            flops=0, transcendentals=0, bytes_accessed=4 * half * rows * width * 2
        ),
        name="order_in",
    )(dp_of, t_of, held, other)
    return [o.reshape(-1, o.shape[2]) for o in outs]


def scatter_blocks(wires, grads, order, parts):
    rows = grads[0].shape[0] // wires.dp_size
    slot_order = order[::-1]
    dp_of, t_of = wires.places(slot_order)
    half = wires.count // 2
    width = sum(cols for cols, _ in parts)

    def body(dp_ref, t_ref, *refs):
        ins, keep, send = refs[:-2], refs[-2], refs[-1]
        step = pl.program_id(0)

        def put(out):
            at = 0
            for (cols, _), src in zip(parts, ins):
                out[0, :, at : at + cols] = src[0].astype(BF)
                at += cols

        @pl.when(step < half)
        def _():
            put(keep)

        @pl.when(step >= half)
        def _():
            put(send)

    in_specs, views = [], []
    for (cols, split), grad in zip(parts, grads):
        if split:
            in_specs.append(pl.BlockSpec((1, rows, cols), lambda i, d, t: (d[i], 0, t[i])))
        else:
            in_specs.append(pl.BlockSpec((1, rows, cols), lambda i, d, t: (d[i], 0, 0)))
        views.append(grad.reshape(wires.dp_size, rows, -1))
    keep, send = pl.pallas_call(
        body,
        grid_spec=pltpu.PrefetchScalarGridSpec(
            num_scalar_prefetch=2,
            grid=(2 * half,),
            in_specs=in_specs,
            out_specs=[
                pl.BlockSpec((1, rows, width), lambda i, d, t: (jnp.minimum(i, half - 1), 0, 0)),
                pl.BlockSpec((1, rows, width), lambda i, d, t: (jnp.maximum(i - half, 0), 0, 0)),
            ],
        ),
        out_shape=[jax.ShapeDtypeStruct((half, rows, width), BF)] * 2,
        cost_estimate=pl.CostEstimate(
            flops=0, transcendentals=0, bytes_accessed=2 * half * rows * width * 6
        ),
        name="order_out",
    )(dp_of, t_of, *views)
    for bit in order[:-1]:
        got = wires.swap(send, bit)
        half = keep.shape[0] // 2
        send = (keep[half:].astype(F32) + got[half:].astype(F32)).astype(BF)
        keep = (keep[:half].astype(F32) + got[:half].astype(F32)).astype(BF)
    got = wires.swap(send, order[-1])
    return (keep.astype(F32) + got.astype(F32))[0]


BLOCK = 256


def visible_t(bq_row, bk_col, span, block):
    key = lax.broadcasted_iota(jnp.int32, (span, block), 0) - WINDOW
    query = lax.broadcasted_iota(jnp.int32, (span, block), 1)
    distance = query - key
    return (distance >= 0) & (distance < WINDOW) & (bq_row == bk_col)


def attend_fwd_body(heads, block, q_ref, k_ref, v_ref, bq_ref, bk_ref, out_ref):
    span = block + WINDOW
    first = pl.multiple_of(pl.program_id(0) * block, block)
    keys = k_ref[pl.ds(first, span), :]
    vals = v_ref[pl.ds(first, span), :]
    key = lax.broadcasted_iota(jnp.int32, (block, span), 1) - WINDOW
    query = lax.broadcasted_iota(jnp.int32, (block, span), 0)
    distance = query - key
    bk = bk_ref[:, pl.ds(first, span)]
    seen = (distance >= 0) & (distance < WINDOW) & (bq_ref[...] == bk)
    for h in range(heads):
        scores = dot_nt(q_ref[:, h * HD : (h + 1) * HD], keys)
        weight = jnp.where(seen, jnp.exp(scores), 0.0)
        total = jnp.sum(weight, axis=1, keepdims=True)
        mixed = dot(weight.astype(BF), vals) / total
        out_ref[:, h * HD : (h + 1) * HD] = mixed.astype(BF)


def attend_bwd_body(heads, block, q_ref, k_ref, v_ref, do_ref, bq_ref, bk_ref, dq_ref, dk_ref, dv_ref):
    span = block + WINDOW
    step = pl.program_id(0)
    first = pl.multiple_of(step * block, block)

    @pl.when(step == 0)
    def _():
        dk_ref[...] = jnp.zeros_like(dk_ref)
        dv_ref[...] = jnp.zeros_like(dv_ref)

    keys = k_ref[pl.ds(first, span), :]
    vals = v_ref[pl.ds(first, span), :]
    seen = visible_t(bq_ref[...], bk_ref[pl.ds(first, span), :], span, block)
    dk = jnp.zeros((span, HD), F32)
    dv = jnp.zeros((span, HD), F32)
    for h in range(heads):
        q = q_ref[:, h * HD : (h + 1) * HD]
        do = do_ref[:, h * HD : (h + 1) * HD]
        weight = jnp.where(seen, jnp.exp(dot_nt(keys, q)), 0.0)
        inv = 1.0 / jnp.sum(weight, axis=0, keepdims=True)
        probs = weight * inv
        dprobs = dot_nt(vals, do)
        inner = jnp.sum(probs * dprobs, axis=0, keepdims=True)
        dscores = (probs * (dprobs - inner)).astype(BF)
        dv = dv + dot(probs.astype(BF), do)
        dk = dk + dot(dscores, q)
        dq_ref[:, h * HD : (h + 1) * HD] = dot_tn(dscores, keys) * (HD**-0.5)
    dk_ref[pl.ds(first, span), :] += dk
    dv_ref[pl.ds(first, span), :] += dv


def attend_forward(q, k, v, bq, bk):
    rows, width = q.shape
    heads = width // HD
    total = k.shape[0]
    block = min(BLOCK, rows)
    flops = 4 * rows * width * (block + WINDOW)
    return pl.pallas_call(
        functools.partial(attend_fwd_body, heads, block),
        grid=(rows // block,),
        in_specs=[
            pl.BlockSpec((block, width), lambda i: (i, 0)),
            pl.BlockSpec((total, HD), lambda i: (0, 0)),
            pl.BlockSpec((total, HD), lambda i: (0, 0)),
            pl.BlockSpec((block, 1), lambda i: (i, 0)),
            pl.BlockSpec((1, total), lambda i: (0, 0)),
        ],
        out_specs=pl.BlockSpec((block, width), lambda i: (i, 0)),
        out_shape=jax.ShapeDtypeStruct((rows, width), BF),
        cost_estimate=pl.CostEstimate(flops=flops, transcendentals=0, bytes_accessed=rows * width * 4),
        name="attend_fwd",
    )(q, k, v, bq[:, None], bk[None, :])


def attend_backward(q, k, v, do, bq, bk):
    rows, width = q.shape
    heads = width // HD
    total = k.shape[0]
    block = min(BLOCK, rows)
    flops = 10 * rows * width * (block + WINDOW)
    return pl.pallas_call(
        functools.partial(attend_bwd_body, heads, block),
        grid=(rows // block,),
        in_specs=[
            pl.BlockSpec((block, width), lambda i: (i, 0)),
            pl.BlockSpec((total, HD), lambda i: (0, 0)),
            pl.BlockSpec((total, HD), lambda i: (0, 0)),
            pl.BlockSpec((block, width), lambda i: (i, 0)),
            pl.BlockSpec((1, block), lambda i: (0, i)),
            pl.BlockSpec((total, 1), lambda i: (0, 0)),
        ],
        out_specs=[
            pl.BlockSpec((block, width), lambda i: (i, 0)),
            pl.BlockSpec((total, HD), lambda i: (0, 0)),
            pl.BlockSpec((total, HD), lambda i: (0, 0)),
        ],
        out_shape=[
            jax.ShapeDtypeStruct((rows, width), F32),
            jax.ShapeDtypeStruct((total, HD), F32),
            jax.ShapeDtypeStruct((total, HD), F32),
        ],
        cost_estimate=pl.CostEstimate(flops=flops, transcendentals=0, bytes_accessed=rows * width * 8),
        name="attend_bwd",
    )(q, k, v, do, bq[None, :], bk[:, None])


def shards(
    dp_size,
    tensor_size,
    tokens_in,
    positions,
    gain_attn_in,
    w_query,
    w_key,
    w_value,
    gain_query,
    gain_key,
    w_output,
    gain_attn_post,
    gain_ff_in,
    w_gate,
    w_up,
    w_down,
    gain_ff_post,
    cotangent,
):
    wires = Wires(dp_size, tensor_size)
    order_a, order_b = wires.orders()
    mine = lax.axis_index("tensor")
    rows = tokens_in.shape[0]
    shard_rows, hq_cols = w_query.shape
    ff_cols = w_gate.shape[1]
    kv_cols = HD // tensor_size
    head_rows = gain_query.shape[0]
    lanes = 128

    forward_ring = [(i, i + 1) for i in range(tensor_size - 1)]
    backward_ring = [(i + 1, i) for i in range(tensor_size - 1)]
    halo = lax.ppermute(tokens_in[rows - WINDOW :], "tensor", forward_ring)

    def column(gain):
        return jnp.pad(gain[:, None], ((0, shard_rows - gain.shape[0]), (0, 0)))

    gains = jnp.concatenate(
        [column(g) for g in (gain_attn_in, gain_attn_post, gain_ff_in, gain_ff_post, gain_query, gain_key)],
        axis=1,
    )
    gains = jnp.pad(gains, ((0, 0), (0, lanes - gains.shape[1])))
    pack_qkv = jnp.concatenate(
        [
            w_query,
            lax.dynamic_slice_in_dim(w_key, mine * kv_cols, kv_cols, 1),
            lax.dynamic_slice_in_dim(w_value, mine * kv_cols, kv_cols, 1),
            gains,
        ],
        axis=1,
    )
    w_q, w_k, w_v, gains_full = gather_blocks(
        wires, pack_qkv, order_a, ((hq_cols, True), (kv_cols, True), (kv_cols, True), (lanes, False))
    )
    (w_o_t,) = gather_blocks(wires, w_output.T, order_b, ((hq_cols, True),))
    (w_g,) = gather_blocks(wires, w_gate, order_a, ((ff_cols, True),))
    (w_u,) = gather_blocks(wires, w_up, order_b, ((ff_cols, True),))
    (w_d_t,) = gather_blocks(wires, w_down.T, order_a, ((ff_cols, True),))
    gain_in_full, post_gain, ff_gain, ff_post_gain = (gains_full[:, j].astype(F32) for j in range(4))
    head_gains = gains_full.reshape(dp_size, shard_rows, lanes)[:, :head_rows].reshape(HD, lanes)
    query_gain, key_gain = (head_gains[:, j].astype(F32) for j in (4, 5))

    start = mine * rows
    base = positions - jnp.arange(positions.shape[0], dtype=jnp.int32)
    none = jnp.full((WINDOW,), -(2**30), jnp.int32)
    base_ext = lax.dynamic_slice_in_dim(jnp.concatenate([none, base]), start, rows + WINDOW)
    places_ext = lax.dynamic_slice_in_dim(
        jnp.concatenate([jnp.zeros((WINDOW,), jnp.int32), positions]), start, rows + WINDOW
    )
    base_own = base_ext[WINDOW:]
    cosine, sine = rope_tables(places_ext)
    head_count = hq_cols * tensor_size // HD

    inputs_ext = jnp.concatenate([halo, tokens_in], axis=0).astype(F32)
    inputs = tokens_in.astype(F32)
    normed_f, in_back = jax.vjp(rms_norm, inputs_ext, gain_in_full)
    normed_ext = normed_f.astype(BF)
    normed = normed_ext[WINDOW:]
    query_raw = dot(normed, w_q)
    key_raw = dot(normed_ext, w_k)
    value = dot(normed_ext, w_v).astype(BF)

    def prep_query(raw_rows, scale_gain):
        shaped = raw_rows.reshape(rows, head_count, HD)
        return rotate(
            rms_norm(shaped, scale_gain), cosine[WINDOW:, None, :], sine[WINDOW:, None, :]
        ).reshape(rows, head_count * HD)

    def prep_key(raw_rows, scale_gain):
        return rotate(rms_norm(raw_rows, scale_gain), cosine, sine)

    query_rot, query_back = jax.vjp(prep_query, query_raw, query_gain)
    key_rot, key_back = jax.vjp(prep_key, key_raw, key_gain)
    query_low = (query_rot * (HD**-0.5)).astype(BF)
    key_low = key_rot.astype(BF)
    mixed = attend_forward(query_low, key_low, value, base_own, base_ext)
    branch = dot_nt(mixed, w_o_t)
    attn_term, post_back = jax.vjp(rms_norm, branch, post_gain)
    middle = inputs + attn_term
    normed_ff_f, ff_in_back = jax.vjp(rms_norm, middle, ff_gain)
    normed_ff = normed_ff_f.astype(BF)
    gate_vals = dot(normed_ff, w_g)
    up_vals = dot(normed_ff, w_u)
    hidden_f, act_back = jax.vjp(geglu, gate_vals, up_vals)
    hidden = hidden_f.astype(BF)
    branch_ff = dot_nt(hidden, w_d_t)
    ff_term, ff_post_back = jax.vjp(rms_norm, branch_ff, ff_post_gain)
    result = (middle + ff_term).astype(BF)

    grad_out = cotangent.astype(F32)
    grad_branch_ff, grad_ff_post = ff_post_back(grad_out)
    grad_ff_rows = grad_branch_ff.astype(BF)
    grad_down_t = dot_tn(grad_ff_rows, hidden)
    grad_hidden = dot(grad_ff_rows, w_d_t)
    grad_gate_f, grad_up_f = act_back(grad_hidden)
    grad_gate = grad_gate_f.astype(BF)
    grad_up = grad_up_f.astype(BF)
    grad_gate_w = dot_tn(normed_ff, grad_gate)
    grad_up_w = dot_tn(normed_ff, grad_up)
    scatter_a, scatter_b = order_a[::-1], order_b[::-1]
    part_down = scatter_blocks(wires, [grad_down_t], scatter_a, ((ff_cols, True),))
    part_gate = scatter_blocks(wires, [grad_gate_w], scatter_b, ((ff_cols, True),))
    part_up = scatter_blocks(wires, [grad_up_w], scatter_a, ((ff_cols, True),))
    grad_normed_ff = dot_nt(grad_gate, w_g) + dot_nt(grad_up, w_u)
    grad_middle_ff, grad_ff_gain = ff_in_back(grad_normed_ff)
    grad_middle = grad_out + grad_middle_ff
    grad_branch, grad_post_gain = post_back(grad_middle)
    grad_branch_rows = grad_branch.astype(BF)
    grad_output_t = dot_tn(grad_branch_rows, mixed)
    part_output = scatter_blocks(wires, [grad_output_t], scatter_b, ((hq_cols, True),))
    grad_mixed = dot(grad_branch_rows, w_o_t).astype(BF)
    grad_query_rot, grad_key_rot, grad_value_rows = attend_backward(
        query_low, key_low, value, grad_mixed, base_own, base_ext
    )
    grad_query_raw, grad_query_gain = query_back(grad_query_rot)
    grad_key_raw, grad_key_gain = key_back(grad_key_rot)
    grad_query_low = grad_query_raw.astype(BF)
    grad_key_low = grad_key_raw.astype(BF)
    grad_value_low = grad_value_rows.astype(BF)
    grad_query_w = dot_tn(normed, grad_query_low)
    grad_key_w = dot_tn(normed_ext, grad_key_low)
    grad_value_w = dot_tn(normed_ext, grad_value_low)
    grad_normed = dot_nt(grad_key_low, w_k) + dot_nt(grad_value_low, w_v)
    grad_normed = grad_normed + jnp.pad(dot_nt(grad_query_low, w_q), ((WINDOW, 0), (0, 0)))
    grad_inputs, grad_gain_in = in_back(grad_normed)
    grad_halo = lax.ppermute(grad_inputs[:WINDOW].astype(BF), "tensor", backward_ring)
    grad_tokens = grad_middle + grad_inputs[WINDOW:]
    grad_tokens = grad_tokens + jnp.pad(grad_halo.astype(F32), ((rows - WINDOW, 0), (0, 0)))

    def head_column(grad):
        spread = jnp.pad(grad.reshape(dp_size, head_rows), ((0, 0), (0, shard_rows - head_rows)))
        return spread.reshape(dp_size * shard_rows)

    gain_grads = jnp.stack(
        [
            grad_gain_in,
            grad_post_gain,
            grad_ff_gain,
            grad_ff_post,
            head_column(grad_query_gain),
            head_column(grad_key_gain),
        ],
        axis=1,
    )
    gain_grads = jnp.pad(gain_grads, ((0, 0), (0, lanes - gain_grads.shape[1])))
    part_last = scatter_blocks(
        wires,
        [grad_query_w, grad_key_w, grad_value_w, gain_grads],
        scatter_b,
        ((hq_cols, True), (HD, False), (HD, False), (lanes, False)),
    )
    at = hq_cols + 2 * HD
    return (
        result,
        grad_tokens,
        part_last[:, at],
        part_last[:, :hq_cols],
        part_last[:, hq_cols : hq_cols + HD],
        part_last[:, hq_cols + HD : at],
        part_last[:head_rows, at + 4],
        part_last[:head_rows, at + 5],
        part_output.T,
        part_last[:, at + 1],
        part_last[:, at + 2],
        part_gate,
        part_up,
        part_down.T,
        part_last[:, at + 3],
    )


def solution(mesh):
    in_specs = (
        P(("dp", "tensor"), None),
        P("dp"),
        P("dp"),
        P("dp", "tensor"),
        P("dp", None),
        P("dp", None),
        P("dp"),
        P("dp"),
        P("tensor", "dp"),
        P("dp"),
        P("dp"),
        P("dp", "tensor"),
        P("dp", "tensor"),
        P("tensor", "dp"),
        P("dp"),
        P(("dp", "tensor"), None),
    )
    out_specs = (
        P(("dp", "tensor"), None),
        P(("dp", "tensor"), None),
        P("dp"),
        P("dp", "tensor"),
        P("dp", None),
        P("dp", None),
        P("dp"),
        P("dp"),
        P("tensor", "dp"),
        P("dp"),
        P("dp"),
        P("dp", "tensor"),
        P("dp", "tensor"),
        P("tensor", "dp"),
        P("dp"),
    )
    body = functools.partial(shards, mesh.shape["dp"], mesh.shape["tensor"])
    return jax.shard_map(body, mesh=mesh, in_specs=in_specs, out_specs=out_specs, check_vma=False)
```

```python
import functools
import math

import jax
import jax.numpy as jnp
from jax import lax
from jax.experimental import pallas as pl
from jax.experimental.pallas import tpu as pltpu
from jax.sharding import PartitionSpec as P

HD = 256
WINDOW = 512
NORM_EPS = 1e-06
ROPE_BASE = 10000.0
BF = jnp.bfloat16
F32 = jnp.float32


def rope_tables(places):
    freq_index = jnp.arange(HD // 2, dtype=F32)
    inverse = jnp.exp(freq_index * (-2.0 * math.log(ROPE_BASE) / HD))
    angles = places.astype(F32)[:, None] * inverse[None, :]
    return (jnp.cos(angles), jnp.sin(angles))


def dot(a, b):
    return jnp.dot(a, b, preferred_element_type=F32)


def dot_nt(a, b):
    return lax.dot_general(a, b, (((1,), (1,)), ((), ())), preferred_element_type=F32)


def dot_tn(a, b):
    return lax.dot_general(a, b, (((0,), (0,)), ((), ())), preferred_element_type=F32)


class Wires:
    def __init__(self, dp_size, tensor_size):
        self.dp_size = dp_size
        self.tensor_size = tensor_size
        self.dp_bits = dp_size.bit_length() - 1
        self.t_bits = tensor_size.bit_length() - 1
        self.count = dp_size * tensor_size

    def swap(self, values, bit):
        axis, size, mask = bit[0], self.dp_size, 1 << bit[1]
        if axis == "tensor":
            size = self.tensor_size
        return lax.ppermute(values, axis, [(i, i ^ mask) for i in range(size)])

    def orders(self):
        far = [("dp", b) for b in range(self.dp_bits - 1, 1, -1)]
        near = [("dp", 1)] if self.dp_bits > 1 else []
        core = [("dp", 0)] if self.dp_bits > 0 else []
        cross = [("tensor", b) for b in range(self.t_bits)]
        return far + near + cross + core, far + cross + near + core

    def places(self, order):
        slot = jnp.arange(self.count, dtype=jnp.int32)
        dp_rel = jnp.zeros_like(slot)
        t_rel = jnp.zeros_like(slot)
        for position, (axis, b) in enumerate(order):
            value = ((slot >> position) & 1) << b
            if axis == "dp":
                dp_rel = dp_rel | value
            else:
                t_rel = t_rel | value
        return (
            dp_rel ^ lax.axis_index("dp").astype(jnp.int32),
            t_rel ^ lax.axis_index("tensor").astype(jnp.int32),
        )


def gather_steps(wires, groups):
    held = [block[None] for block, _ in groups]
    others = [None] * len(groups)
    for k in range(len(groups[0][1])):
        lead = None
        for g, (_, order) in enumerate(groups):
            send = held[g]
            if lead is not None:
                send, _ = lax.optimization_barrier((send, lead))
            got = wires.swap(send, order[k])
            if g == 0 or k < 2:
                lead = got
            if k + 1 < len(order):
                held[g] = jnp.concatenate([held[g], got], axis=0)
            else:
                others[g] = got
    return list(zip(held, others))


def in_order(wires, pair, order, parts):
    dp_of, t_of = wires.places(order)
    held, other = pair
    half, rows, width = held.shape

    def body(dp_ref, t_ref, a_ref, b_ref, *outs):
        def put(src, slot, index):
            d, t = dp_ref[slot], t_ref[slot]
            at = 0
            for (cols, split), out in zip(parts, outs):
                where = pl.ds(pl.multiple_of(t * cols, cols), cols) if split else pl.ds(0, cols)
                out[d, :, where] = src[index, :, at : at + cols]
                at += cols

        @pl.loop(0, half)
        def _(i):
            put(a_ref, i, i)
            put(b_ref, i + half, i)

    out_shape = []
    for cols, split in parts:
        wide = cols * wires.tensor_size if split else cols
        out_shape.append(jax.ShapeDtypeStruct((wires.dp_size, rows, wide), held.dtype))
    vmem, smem = pl.BlockSpec(memory_space=pltpu.VMEM), pl.BlockSpec(memory_space=pltpu.SMEM)
    outs = pl.pallas_call(
        body,
        in_specs=[smem, smem, vmem, vmem],
        out_specs=[vmem] * len(parts),
        out_shape=out_shape,
        cost_estimate=pl.CostEstimate(
            flops=0, transcendentals=0, bytes_accessed=4 * half * rows * width * 2
        ),
        name="order_in",
    )(dp_of, t_of, held, other)
    return [o.reshape(-1, o.shape[2]) for o in outs]


def scatter_start(wires, grads, order, parts):
    rows = grads[0].shape[0] // wires.dp_size
    dp_of, t_of = wires.places(order[::-1])
    half = wires.count // 2
    width = sum(cols for cols, _ in parts)

    def body(dp_ref, t_ref, *refs):
        ins, keep, send = refs[:-2], refs[-2], refs[-1]

        def put(out, slot, index):
            d, t = dp_ref[slot], t_ref[slot]
            at = 0
            for (cols, split), src in zip(parts, ins):
                where = pl.ds(pl.multiple_of(t * cols, cols), cols) if split else pl.ds(0, cols)
                out[index, :, at : at + cols] = src[d, :, where].astype(BF)
                at += cols

        @pl.loop(0, half)
        def _(i):
            put(keep, i, i)
            put(send, i + half, i)

    views = [grad.reshape(wires.dp_size, rows, -1) for grad in grads]
    vmem, smem = pl.BlockSpec(memory_space=pltpu.VMEM), pl.BlockSpec(memory_space=pltpu.SMEM)
    keep, send = pl.pallas_call(
        body,
        in_specs=[smem, smem] + [vmem] * len(parts),
        out_specs=[vmem, vmem],
        out_shape=[jax.ShapeDtypeStruct((half, rows, width), BF)] * 2,
        cost_estimate=pl.CostEstimate(
            flops=0, transcendentals=0, bytes_accessed=2 * half * rows * width * 6
        ),
        name="order_out",
    )(dp_of, t_of, *views)
    return scatter_add(keep, wires.swap(send, order[0]))


def scatter_add(keep, got):
    half = keep.shape[0] // 2
    send = (keep[half:].astype(F32) + got[half:].astype(F32)).astype(BF)
    keep = (keep[:half].astype(F32) + got[:half].astype(F32)).astype(BF)
    return keep, send


def scatter_rest(wires, keep, send, order):
    for bit in order[1:-1]:
        keep, send = scatter_add(keep, wires.swap(send, bit))
    got = wires.swap(send, order[-1])
    return (keep.astype(F32) + got.astype(F32))[0]


BLOCK = 256


def visible_t(bq_row, bk_col, span, block):
    key = lax.broadcasted_iota(jnp.int32, (span, block), 0) - WINDOW
    query = lax.broadcasted_iota(jnp.int32, (span, block), 1)
    distance = query - key
    return (distance >= 0) & (distance < WINDOW) & (bq_row == bk_col)


def attend_fwd_body(heads, block, q_ref, k_ref, v_ref, bq_ref, bk_ref, out_ref):
    span = block + WINDOW
    first = pl.multiple_of(pl.program_id(0) * block, block)
    keys = k_ref[pl.ds(first, span), :]
    vals = v_ref[pl.ds(first, span), :]
    key = lax.broadcasted_iota(jnp.int32, (block, span), 1) - WINDOW
    query = lax.broadcasted_iota(jnp.int32, (block, span), 0)
    distance = query - key
    bk = bk_ref[:, pl.ds(first, span)]
    seen = (distance >= 0) & (distance < WINDOW) & (bq_ref[...] == bk)
    for h in range(heads):
        scores = dot_nt(q_ref[:, h * HD : (h + 1) * HD], keys)
        weight = jnp.where(seen, jnp.exp(scores), 0.0)
        total = jnp.sum(weight, axis=1, keepdims=True)
        mixed = dot(weight.astype(BF), vals) / total
        out_ref[:, h * HD : (h + 1) * HD] = mixed.astype(BF)


def attend_bwd_body(heads, block, q_ref, k_ref, v_ref, do_ref, bq_ref, bk_ref, dq_ref, dk_ref, dv_ref):
    span = block + WINDOW
    step = pl.program_id(0)
    first = pl.multiple_of(step * block, block)

    @pl.when(step == 0)
    def _():
        dk_ref[...] = jnp.zeros_like(dk_ref)
        dv_ref[...] = jnp.zeros_like(dv_ref)

    keys = k_ref[pl.ds(first, span), :]
    vals = v_ref[pl.ds(first, span), :]
    seen = visible_t(bq_ref[...], bk_ref[pl.ds(first, span), :], span, block)
    dk = jnp.zeros((span, HD), F32)
    dv = jnp.zeros((span, HD), F32)
    for h in range(heads):
        q = q_ref[:, h * HD : (h + 1) * HD]
        do = do_ref[:, h * HD : (h + 1) * HD]
        weight = jnp.where(seen, jnp.exp(dot_nt(keys, q)), 0.0)
        inv = 1.0 / jnp.sum(weight, axis=0, keepdims=True)
        probs = weight * inv
        dprobs = dot_nt(vals, do)
        inner = jnp.sum(probs * dprobs, axis=0, keepdims=True)
        dscores = (probs * (dprobs - inner)).astype(BF)
        dv = dv + dot(probs.astype(BF), do)
        dk = dk + dot(dscores, q)
        dq_ref[:, h * HD : (h + 1) * HD] = dot_tn(dscores, keys) * (HD**-0.5)
    dk_ref[pl.ds(first, span), :] += dk
    dv_ref[pl.ds(first, span), :] += dv


def attend_forward(q, k, v, bq, bk):
    rows, width = q.shape
    heads = width // HD
    total = k.shape[0]
    block = min(BLOCK, rows)
    flops = 4 * rows * width * (block + WINDOW)
    return pl.pallas_call(
        functools.partial(attend_fwd_body, heads, block),
        grid=(rows // block,),
        in_specs=[
            pl.BlockSpec((block, width), lambda i: (i, 0)),
            pl.BlockSpec((total, HD), lambda i: (0, 0)),
            pl.BlockSpec((total, HD), lambda i: (0, 0)),
            pl.BlockSpec((block, 1), lambda i: (i, 0)),
            pl.BlockSpec((1, total), lambda i: (0, 0)),
        ],
        out_specs=pl.BlockSpec((block, width), lambda i: (i, 0)),
        out_shape=jax.ShapeDtypeStruct((rows, width), BF),
        cost_estimate=pl.CostEstimate(flops=flops, transcendentals=0, bytes_accessed=rows * width * 4),
        name="attend_fwd",
    )(q, k, v, bq[:, None], bk[None, :])


def attend_backward(q, k, v, do, bq, bk):
    rows, width = q.shape
    heads = width // HD
    total = k.shape[0]
    block = min(BLOCK, rows)
    flops = 10 * rows * width * (block + WINDOW)
    return pl.pallas_call(
        functools.partial(attend_bwd_body, heads, block),
        grid=(rows // block,),
        in_specs=[
            pl.BlockSpec((block, width), lambda i: (i, 0)),
            pl.BlockSpec((total, HD), lambda i: (0, 0)),
            pl.BlockSpec((total, HD), lambda i: (0, 0)),
            pl.BlockSpec((block, width), lambda i: (i, 0)),
            pl.BlockSpec((1, block), lambda i: (0, i)),
            pl.BlockSpec((total, 1), lambda i: (0, 0)),
        ],
        out_specs=[
            pl.BlockSpec((block, width), lambda i: (i, 0)),
            pl.BlockSpec((total, HD), lambda i: (0, 0)),
            pl.BlockSpec((total, HD), lambda i: (0, 0)),
        ],
        out_shape=[
            jax.ShapeDtypeStruct((rows, width), F32),
            jax.ShapeDtypeStruct((total, HD), F32),
            jax.ShapeDtypeStruct((total, HD), F32),
        ],
        cost_estimate=pl.CostEstimate(flops=flops, transcendentals=0, bytes_accessed=rows * width * 8),
        name="attend_bwd",
    )(q, k, v, do, bq[None, :], bk[:, None])


GELU_A = 0.044715
GELU_C = math.sqrt(2.0 / math.pi)


def inverse_rms(v):
    return lax.rsqrt(jnp.mean(v * v, axis=-1, keepdims=True) + NORM_EPS)


def rms_back(hat, r, gain, dy):
    scaled = dy * gain
    dv = r * (scaled - hat * jnp.mean(scaled * hat, axis=-1, keepdims=True))
    return dv, jnp.sum(dy * hat, axis=0, keepdims=True)


def turn(u, cos, sin):
    u1, u2 = u[:, : HD // 2], u[:, HD // 2 :]
    return jnp.concatenate([u1 * cos - u2 * sin, u2 * cos + u1 * sin], axis=1)


def turn_back(d, cos, sin):
    d1, d2 = d[:, : HD // 2], d[:, HD // 2 :]
    return jnp.concatenate([d1 * cos + d2 * sin, d2 * cos - d1 * sin], axis=1)


def qkv_fwd_body(
    heads, before, x_ref, gin_ref, gq_ref, gk_ref, wq_ref, wk_ref, wv_ref, cos_ref, sin_ref,
    normed_ref, q_ref, k_ref, v_ref,
):
    x = x_ref[...].astype(F32)
    normed = (x * inverse_rms(x) * gin_ref[...]).astype(BF)
    normed_ref[...] = normed
    cos, sin = cos_ref[...], sin_ref[...]
    v_ref[...] = dot(normed, wv_ref[...]).astype(BF)
    key_raw = dot(normed, wk_ref[...])
    k_ref[...] = turn(key_raw * inverse_rms(key_raw) * gk_ref[...], cos, sin).astype(BF)

    @pl.when(pl.program_id(0) >= before)
    def _():
        for h in range(heads):
            cols = slice(h * HD, (h + 1) * HD)
            raw = dot(normed, wq_ref[:, cols])
            q = turn(raw * inverse_rms(raw) * gq_ref[...], cos, sin)
            q_ref[:, cols] = (q * (HD**-0.5)).astype(BF)


def qkv_bwd_body(
    heads, before, x_ref, gin_ref, gq_ref, gk_ref, wq_ref, wk_ref, wv_ref, cos_ref, sin_ref,
    normed_ref, dq_ref, dk_ref, dv_ref, gmid_ref,
    gtok_ref, ghalo_ref, dwq_ref, dwk_ref, dwv_ref, dgin_ref, dgq_ref, dgk_ref,
):
    step = pl.program_id(0)

    @pl.when(step == 0)
    def _():
        for ref in (dwq_ref, dwk_ref, dwv_ref, dgin_ref, dgq_ref, dgk_ref):
            ref[...] = jnp.zeros_like(ref)

    cos, sin = cos_ref[...], sin_ref[...]
    normed = normed_ref[...]
    key_raw = dot(normed, wk_ref[...])
    r = inverse_rms(key_raw)
    dkey, dgk = rms_back(key_raw * r, r, gk_ref[...], turn_back(dk_ref[...], cos, sin))
    dgk_ref[...] += dgk
    dkey = dkey.astype(BF)
    dval = dv_ref[...].astype(BF)
    dwk_ref[...] += dot_tn(normed, dkey)
    dwv_ref[...] += dot_tn(normed, dval)
    dnormed = dot_nt(dkey, wk_ref[...]) + dot_nt(dval, wv_ref[...])
    x = x_ref[...].astype(F32)
    rx = inverse_rms(x)

    @pl.when(step < before)
    def _():
        dx, dgin = rms_back(x * rx, rx, gin_ref[...], dnormed)
        dgin_ref[...] += dgin
        ghalo_ref[...] = dx.astype(BF)

    @pl.when(step >= before)
    def _():
        total = dnormed
        for h in range(heads):
            cols = slice(h * HD, (h + 1) * HD)
            raw = dot(normed, wq_ref[:, cols])
            rq = inverse_rms(raw)
            dquery, dgq = rms_back(raw * rq, rq, gq_ref[...], turn_back(dq_ref[:, cols], cos, sin))
            dgq_ref[...] += dgq
            dquery = dquery.astype(BF)
            dwq_ref[:, cols] += dot_tn(normed, dquery)
            total = total + dot_nt(dquery, wq_ref[:, cols])
        dx, dgin = rms_back(x * rx, rx, gin_ref[...], total)
        dgin_ref[...] += dgin
        gtok_ref[...] = gmid_ref[...] + dx


def ff_body(
    x_ref, cot_ref, mixed_ref, gpost_ref, gff_ref, gffpost_ref, wo_ref, wg_ref, wu_ref, wd_ref,
    out_ref, gmid_ref, gmixed_ref, dwo_ref, dwg_ref, dwu_ref, dwd_ref, dgpost_ref, dgff_ref, dgffpost_ref,
):
    @pl.when(pl.program_id(0) == 0)
    def _():
        for ref in (dwo_ref, dwg_ref, dwu_ref, dwd_ref, dgpost_ref, dgff_ref, dgffpost_ref):
            ref[...] = jnp.zeros_like(ref)

    mixed = mixed_ref[...]
    branch = dot_nt(mixed, wo_ref[...])
    r_post = inverse_rms(branch)
    hat_post = branch * r_post
    middle = x_ref[...].astype(F32) + hat_post * gpost_ref[...]
    r_ff = inverse_rms(middle)
    hat_ff = middle * r_ff
    normed = (hat_ff * gff_ref[...]).astype(BF)
    gate = dot(normed, wg_ref[...])
    up = dot(normed, wu_ref[...])
    square = gate * gate
    tanh = jnp.tanh(GELU_C * (gate * (1.0 + GELU_A * square)))
    half = 0.5 * (1.0 + tanh)
    act = gate * half
    slope = half + (0.5 * GELU_C) * gate * (1.0 - tanh * tanh) * (1.0 + (3.0 * GELU_A) * square)
    hidden = (act * up).astype(BF)
    branch_ff = dot_nt(hidden, wd_ref[...])
    r_ffpost = inverse_rms(branch_ff)
    hat_ffpost = branch_ff * r_ffpost
    out_ref[...] = (middle + hat_ffpost * gffpost_ref[...]).astype(BF)

    dout = cot_ref[...].astype(F32)
    dbranch_ff, dg = rms_back(hat_ffpost, r_ffpost, gffpost_ref[...], dout)
    dgffpost_ref[...] += dg
    dbranch_ff = dbranch_ff.astype(BF)
    dwd_ref[...] += dot_tn(dbranch_ff, hidden)
    dhidden = dot(dbranch_ff, wd_ref[...])
    dgate = (dhidden * up * slope).astype(BF)
    dup = (dhidden * act).astype(BF)
    dwg_ref[...] += dot_tn(normed, dgate)
    dwu_ref[...] += dot_tn(normed, dup)
    dnormed = dot_nt(dgate, wg_ref[...]) + dot_nt(dup, wu_ref[...])
    dmid, dg = rms_back(hat_ff, r_ff, gff_ref[...], dnormed)
    dgff_ref[...] += dg
    dmid = dout + dmid
    gmid_ref[...] = dmid
    dbranch, dg = rms_back(hat_post, r_post, gpost_ref[...], dmid)
    dgpost_ref[...] += dg
    dbranch = dbranch.astype(BF)
    dwo_ref[...] += dot_tn(dbranch, mixed)
    gmixed_ref[...] = dot(dbranch, wo_ref[...]).astype(BF)


def by_rows(block, width, skip=0, last=None):
    if last is not None:
        return pl.BlockSpec((block, width), lambda i: (jnp.minimum(i, last), 0))
    return pl.BlockSpec((block, width), lambda i: (jnp.maximum(i - skip, 0), 0))


def whole(shape):
    return pl.BlockSpec(shape, lambda i: (0, 0), pipeline_mode=pl.Buffered(1))


def qkv_forward(x_ext, gains, weights, tables):
    total, width = x_ext.shape
    block = min(BLOCK, WINDOW)
    before = WINDOW // block
    hq = weights[0].shape[1]
    rows = total - WINDOW
    flops = 2 * total * width * (hq + 2 * HD)
    return pl.pallas_call(
        functools.partial(qkv_fwd_body, hq // HD, before),
        grid=(total // block,),
        in_specs=[by_rows(block, width)]
        + [whole(g.shape) for g in gains]
        + [whole(w.shape) for w in weights]
        + [by_rows(block, HD // 2)] * 2,
        out_specs=[by_rows(block, width), by_rows(block, hq, before), by_rows(block, HD), by_rows(block, HD)],
        out_shape=[
            jax.ShapeDtypeStruct((total, width), BF),
            jax.ShapeDtypeStruct((rows, hq), BF),
            jax.ShapeDtypeStruct((total, HD), BF),
            jax.ShapeDtypeStruct((total, HD), BF),
        ],
        cost_estimate=pl.CostEstimate(flops=flops, transcendentals=0, bytes_accessed=total * width * 8),
        name="qkv_fwd",
    )(x_ext, *gains, *weights, *tables)


def qkv_backward(x_ext, gains, weights, tables, normed, dq, dk, dv, gmid):
    total, width = x_ext.shape
    block = min(BLOCK, WINDOW)
    before = WINDOW // block
    hq = weights[0].shape[1]
    rows = total - WINDOW
    flops = 6 * total * width * (hq + 2 * HD)
    sums = [(width, hq), (width, HD), (width, HD), (1, width), (1, HD), (1, HD)]
    return pl.pallas_call(
        functools.partial(qkv_bwd_body, hq // HD, before),
        grid=(total // block,),
        in_specs=[by_rows(block, width)]
        + [whole(g.shape) for g in gains]
        + [whole(w.shape) for w in weights]
        + [by_rows(block, HD // 2)] * 2
        + [by_rows(block, width), by_rows(block, hq, before), by_rows(block, HD), by_rows(block, HD)]
        + [by_rows(block, width, before)],
        out_specs=[by_rows(block, width, before), by_rows(block, width, 0, before - 1)]
        + [pl.BlockSpec(shape, lambda i: (0, 0)) for shape in sums],
        out_shape=[jax.ShapeDtypeStruct((rows, width), F32), jax.ShapeDtypeStruct((WINDOW, width), BF)]
        + [jax.ShapeDtypeStruct(shape, F32) for shape in sums],
        cost_estimate=pl.CostEstimate(flops=flops, transcendentals=0, bytes_accessed=total * width * 16),
        name="qkv_bwd",
    )(x_ext, *gains, *weights, *tables, normed, dq, dk, dv, gmid)


def feed_forward(x, cot, mixed, gains, weights):
    rows, width = x.shape
    block = min(BLOCK, rows)
    hq, ff = weights[0].shape[1], weights[1].shape[1]
    flops = 6 * rows * width * (hq + 3 * ff)
    sums = [(width, hq)] + [(width, ff)] * 3 + [(1, width)] * 3
    return pl.pallas_call(
        ff_body,
        grid=(rows // block,),
        in_specs=[by_rows(block, width), by_rows(block, width), by_rows(block, hq)]
        + [whole(g.shape) for g in gains]
        + [whole(w.shape) for w in weights],
        out_specs=[by_rows(block, width), by_rows(block, width), by_rows(block, hq)]
        + [pl.BlockSpec(shape, lambda i: (0, 0), pipeline_mode=pl.Buffered(1)) for shape in sums],
        out_shape=[
            jax.ShapeDtypeStruct((rows, width), BF),
            jax.ShapeDtypeStruct((rows, width), F32),
            jax.ShapeDtypeStruct((rows, hq), BF),
        ]
        + [jax.ShapeDtypeStruct(shape, F32) for shape in sums],
        cost_estimate=pl.CostEstimate(flops=flops, transcendentals=0, bytes_accessed=rows * width * 64),
        compiler_params=pltpu.CompilerParams(vmem_limit_bytes=63 * 2**20),
        name="feed_forward",
    )(x, cot, mixed, *gains, *weights)


def shards(
    dp_size,
    tensor_size,
    tokens_in,
    positions,
    gain_attn_in,
    w_query,
    w_key,
    w_value,
    gain_query,
    gain_key,
    w_output,
    gain_attn_post,
    gain_ff_in,
    w_gate,
    w_up,
    w_down,
    gain_ff_post,
    cotangent,
):
    wires = Wires(dp_size, tensor_size)
    order_a, order_b = wires.orders()
    mine = lax.axis_index("tensor")
    rows = tokens_in.shape[0]
    shard_rows, hq_cols = w_query.shape
    ff_cols = w_gate.shape[1]
    kv_cols = HD // tensor_size
    head_rows = gain_query.shape[0]
    lanes = 128

    forward_ring = [(i, i + 1) for i in range(tensor_size - 1)]
    backward_ring = [(i + 1, i) for i in range(tensor_size - 1)]
    halo = lax.ppermute(tokens_in[rows - WINDOW :], "tensor", forward_ring)

    def column(gain):
        return jnp.pad(gain[:, None], ((0, shard_rows - gain.shape[0]), (0, 0)))

    gains = jnp.concatenate(
        [column(g) for g in (gain_attn_in, gain_attn_post, gain_ff_in, gain_ff_post, gain_query, gain_key)],
        axis=1,
    )
    gains = jnp.pad(gains, ((0, 0), (0, lanes - gains.shape[1])))
    pack_qkv = jnp.concatenate(
        [
            w_query,
            lax.dynamic_slice_in_dim(w_key, mine * kv_cols, kv_cols, 1),
            lax.dynamic_slice_in_dim(w_value, mine * kv_cols, kv_cols, 1),
            gains,
        ],
        axis=1,
    )
    pack_b = jnp.concatenate([w_output.T, w_gate], axis=1)
    pack_c = jnp.concatenate([w_up, w_down.T], axis=1)
    moved = gather_steps(wires, [(pack_qkv, order_a), (pack_b, order_a), (pack_c, order_b)])
    w_q, w_k, w_v, gains_full = in_order(
        wires, moved[0], order_a, ((hq_cols, True), (kv_cols, True), (kv_cols, True), (lanes, False))
    )
    w_o_t, w_g = in_order(wires, moved[1], order_a, ((hq_cols, True), (ff_cols, True)))
    w_u, w_d_t = in_order(wires, moved[2], order_b, ((ff_cols, True), (ff_cols, True)))
    def row(values):
        return values.astype(F32)[None, :]

    gain_in_full, post_gain, ff_gain, ff_post_gain = (row(gains_full[:, j]) for j in range(4))
    head_gains = gains_full.reshape(dp_size, shard_rows, lanes)[:, :head_rows].reshape(HD, lanes)
    query_gain, key_gain = (row(head_gains[:, j]) for j in (4, 5))

    start = mine * rows
    base = positions - jnp.arange(positions.shape[0], dtype=jnp.int32)
    none = jnp.full((WINDOW,), -(2**30), jnp.int32)
    base_ext = lax.dynamic_slice_in_dim(jnp.concatenate([none, base]), start, rows + WINDOW)
    places_ext = lax.dynamic_slice_in_dim(
        jnp.concatenate([jnp.zeros((WINDOW,), jnp.int32), positions]), start, rows + WINDOW
    )
    base_own = base_ext[WINDOW:]
    cosine, sine = rope_tables(places_ext)
    x_ext = jnp.concatenate([halo, tokens_in], axis=0)
    qkv_gains = (gain_in_full, query_gain, key_gain)
    qkv_weights = (w_q, w_k, w_v)
    normed_ext, query_low, key_low, value = qkv_forward(x_ext, qkv_gains, qkv_weights, (cosine, sine))
    mixed = attend_forward(query_low, key_low, value, base_own, base_ext)
    (
        result,
        grad_middle,
        grad_mixed,
        grad_output_t,
        grad_gate_w,
        grad_up_w,
        grad_down_t,
        grad_post_gain,
        grad_ff_gain,
        grad_ff_post,
    ) = feed_forward(
        tokens_in, cotangent, mixed, (post_gain, ff_gain, ff_post_gain), (w_o_t, w_g, w_u, w_d_t)
    )
    scatter_a, scatter_b = order_a[::-1], order_b[::-1]
    first = scatter_start(
        wires, [grad_down_t, grad_gate_w], scatter_a, ((ff_cols, True), (ff_cols, True))
    )
    second = scatter_start(
        wires, [grad_up_w, grad_output_t], scatter_b, ((ff_cols, True), (hq_cols, True))
    )
    grad_mixed, first, second = lax.optimization_barrier((grad_mixed, first, second))
    part_first = scatter_rest(wires, *first, scatter_a)
    part_second = scatter_rest(wires, *second, scatter_b)
    grad_query_rot, grad_key_rot, grad_value_rows = attend_backward(
        query_low, key_low, value, grad_mixed, base_own, base_ext
    )
    (
        grad_tokens,
        grad_halo,
        grad_query_w,
        grad_key_w,
        grad_value_w,
        grad_gain_in,
        grad_query_gain,
        grad_key_gain,
    ) = qkv_backward(
        x_ext,
        qkv_gains,
        qkv_weights,
        (cosine, sine),
        normed_ext,
        grad_query_rot,
        grad_key_rot,
        grad_value_rows,
        grad_middle,
    )
    grad_halo = lax.ppermute(grad_halo, "tensor", backward_ring)
    grad_tokens = grad_tokens + jnp.pad(grad_halo.astype(F32), ((rows - WINDOW, 0), (0, 0)))

    def head_column(grad):
        spread = jnp.pad(grad.reshape(dp_size, head_rows), ((0, 0), (0, shard_rows - head_rows)))
        return spread.reshape(dp_size * shard_rows)

    gain_grads = jnp.stack(
        [
            grad_gain_in[0],
            grad_post_gain[0],
            grad_ff_gain[0],
            grad_ff_post[0],
            head_column(grad_query_gain),
            head_column(grad_key_gain),
        ],
        axis=1,
    )
    gain_grads = jnp.pad(gain_grads, ((0, 0), (0, lanes - gain_grads.shape[1])))
    last = scatter_start(
        wires,
        [grad_query_w, grad_key_w, grad_value_w, gain_grads],
        scatter_b,
        ((hq_cols, True), (HD, False), (HD, False), (lanes, False)),
    )
    part_last = scatter_rest(wires, *last, scatter_b)
    at = hq_cols + 2 * HD
    return (
        result,
        grad_tokens,
        part_last[:, at],
        part_last[:, :hq_cols],
        part_last[:, hq_cols : hq_cols + HD],
        part_last[:, hq_cols + HD : at],
        part_last[:head_rows, at + 4],
        part_last[:head_rows, at + 5],
        part_second[:, ff_cols:].T,
        part_last[:, at + 1],
        part_last[:, at + 2],
        part_first[:, ff_cols:],
        part_second[:, :ff_cols],
        part_first[:, :ff_cols].T,
        part_last[:, at + 3],
    )


def solution(mesh):
    in_specs = (
        P(("dp", "tensor"), None),
        P("dp"),
        P("dp"),
        P("dp", "tensor"),
        P("dp", None),
        P("dp", None),
        P("dp"),
        P("dp"),
        P("tensor", "dp"),
        P("dp"),
        P("dp"),
        P("dp", "tensor"),
        P("dp", "tensor"),
        P("tensor", "dp"),
        P("dp"),
        P(("dp", "tensor"), None),
    )
    out_specs = (
        P(("dp", "tensor"), None),
        P(("dp", "tensor"), None),
        P("dp"),
        P("dp", "tensor"),
        P("dp", None),
        P("dp", None),
        P("dp"),
        P("dp"),
        P("tensor", "dp"),
        P("dp"),
        P("dp"),
        P("dp", "tensor"),
        P("dp", "tensor"),
        P("tensor", "dp"),
        P("dp"),
    )
    body = functools.partial(shards, mesh.shape["dp"], mesh.shape["tensor"])
    return jax.shard_map(body, mesh=mesh, in_specs=in_specs, out_specs=out_specs, check_vma=False)
```
